32 devices in a mesh: dom: 8 (over y, x, core), rep: 4 (over z).
Axes of the slice: x: 2, y: 2, z: 4, core: 2. Of those that a mesh axis runs over, the one named last changes fastest.
Arguments:
- features: bfloat16 [32768, 512], P(('dom', 'rep')), may hold values from -6 to 6
- w_self: bfloat16 [512, 512], replicated, may hold values from -0.25 to 0.25
- w_neigh: bfloat16 [512, 512], replicated, may hold values from -0.25 to 0.25
- local_tiles: bfloat16 [4096, 128, 128], P(('dom', 'rep')), may hold values from -0.09375 to 0.09375
- local_rows: int32 [4096], P(('dom', 'rep')), may hold values from 0 to 7
- local_cols: int32 [4096], P(('dom', 'rep')), may hold values from 0 to 31
- halo_tiles: bfloat16 [3072, 128, 128], P(('dom', 'rep')), may hold values from -0.09375 to 0.09375
- halo_rows: int32 [3072], P(('dom', 'rep')), may hold values from 0 to 7
- halo_cols: int32 [3072], P(('dom', 'rep')), may hold values from 0 to 3
- cut_rows: int32 [8, 4, 8, 64], P('dom', 'rep'), may hold values from 0 to 1023
- cut_counts: int32 [8, 4, 8], P('dom', 'rep'), may hold values from 0 to 64, as said below
- cotangent: bfloat16 [32768, 512], P(('dom', 'rep')), may hold values from -6 to 6
Outputs:
- out: bfloat16 [32768, 512], P(('dom', 'rep'))
- d_x: bfloat16 [32768, 512], P(('dom', 'rep'))
- d_w_self: float32 [512, 512], P('rep')
- d_w_neigh: float32 [512, 512], P('rep')
The draws below stay inside these ranges and needn't reach their ends.
Inputs may be any that keep to these rules, and one draw needn't show every extreme that they name: Each device sends 64 rows to at least one partition and none to its own partition; slots from cut_counts[p, r, q] on are unused.
All inputs are finite; a program needn't handle non-finite values.
Results may differ from the reference program's by a relative error of at most 0.008.
Values may be sent and summed in bfloat16 or wider, within the bound.
No kernel may reach another device: no remote copies, remote signals or barrier semaphores. Data moves between devices by JAX's collectives and lax.ppermute only.
A program may use at most 128 MiB of HBM per device.

```python
import math
import jax
import jax.numpy as jnp
from jax import lax

D = 512
TB = 128
R = 1024
NL = 128
NH = 96
C = 64
RB = 8
PB = 32
HB = 4
NODES = 32768
N_DOM = 8
N_REP = 4


def draw_cut_counts(key, part):
    shape_full = (N_DOM, N_REP, N_DOM)
    drawn = jax.random.randint(key, shape_full, C // 8, C + 1)
    source_part = lax.broadcasted_iota(jnp.int32, shape_full, 0)
    target_part = lax.broadcasted_iota(jnp.int32, shape_full, 2)
    drawn = jnp.where(target_part == (source_part + 1) % N_DOM, C, drawn)
    drawn = jnp.where(target_part == source_part, 0, drawn)
    return drawn.astype(jnp.int32)


def place_ends(entries, own_key, smallest, top_value):
    spot = [jax.random.randint(jax.random.fold_in(own_key, axis), (), 0, length) for axis, length in enumerate(entries.shape)]
    main_axis = entries.shape.index(max(entries.shape))
    beside = spot[:main_axis] + [(spot[main_axis] + 1) % entries.shape[main_axis]] + spot[main_axis + 1:]
    return entries.at[tuple(spot)].set(smallest).at[tuple(beside)].set(top_value)


def levels(key, dims, pieces, smallest, top_value):
    gain = 1.0
    for axis_at, blocks in pieces:
        draws = jax.random.uniform(jax.random.fold_in(jax.random.fold_in(key, 6), axis_at), (blocks,), jnp.float32, smallest / len(pieces), top_value / len(pieces))
        gain = gain * jnp.repeat(jnp.exp(draws), dims[axis_at] // blocks).reshape((-1,) + (1,) * (len(dims) - 1 - axis_at))
    return gain


def scatter_about(stream_key, shape, spread, most, split=(), kind=jnp.bfloat16):
    values = spread * jax.random.normal(stream_key, shape, jnp.float32)
    if split:
        values = values * levels(stream_key, shape, split, -0.22, 0.18)
    return jnp.clip(values, -most, most).astype(kind)


def setup_inputs(seed: int = 0) -> dict:
    streams_of = jax.random.split(jax.random.key(seed), 13)
    return {
        "features": scatter_about(streams_of[0], (NODES, D), 1.0, 6.0, ((0, 32),)),
        "w_self": scatter_about(streams_of[1], (D, D), D ** -0.5, 0.25),
        "w_neigh": scatter_about(streams_of[2], (D, D), D ** -0.5, 0.25),
        "local_tiles": scatter_about(streams_of[3], (N_DOM * N_REP * NL, TB, TB), ((NL + NH) * TB // RB) ** -0.5, 0.09375, ((0, 32),)),
        "local_rows": place_ends(jax.random.randint(streams_of[4], (N_DOM * N_REP * NL,), 0, RB), jax.random.fold_in(streams_of[4], 1), 0, RB - 1).astype(jnp.int32),
        "local_cols": place_ends(jax.random.randint(streams_of[5], (N_DOM * N_REP * NL,), 0, PB), jax.random.fold_in(streams_of[5], 1), 0, PB - 1).astype(jnp.int32),
        "halo_tiles": scatter_about(streams_of[6], (N_DOM * N_REP * NH, TB, TB), ((NL + NH) * TB // RB) ** -0.5, 0.09375, ((0, 32),)),
        "halo_rows": place_ends(jax.random.randint(streams_of[7], (N_DOM * N_REP * NH,), 0, RB), jax.random.fold_in(streams_of[7], 1), 0, RB - 1).astype(jnp.int32),
        "halo_cols": place_ends(jax.random.randint(streams_of[8], (N_DOM * N_REP * NH,), 0, HB), jax.random.fold_in(streams_of[8], 1), 0, HB - 1).astype(jnp.int32),
        "cut_rows": place_ends(jax.random.randint(streams_of[9], (N_DOM, N_REP, N_DOM, C), 0, R), jax.random.fold_in(streams_of[9], 1), 0, R - 1).astype(jnp.int32),
        "cut_counts": draw_cut_counts(jax.random.fold_in(streams_of[12], 71), 0),
        "cotangent": scatter_about(streams_of[11], (NODES, D), 1.0, 6.0, ((0, 32),)),
    }


def aggregate(source, tiles, pick_index, place_index, out_blocks, transposed):
    tile_count = tiles.shape[0]
    group_size = math.gcd(tile_count, 32)
    tile_size = tiles.shape[1]
    feat_width = source.shape[2]
    grouped = tiles.reshape(tile_count // group_size, group_size, tile_size, tile_size)
    picks = pick_index.reshape(tile_count // group_size, group_size)
    places = place_index.reshape(tile_count // group_size, group_size)
    targets = jnp.arange(out_blocks, dtype=jnp.int32)

    def advance(running, scan_item):
        tile_block, pick_group, place_group = scan_item
        picked = jnp.take(source, pick_group, axis=0).astype(jnp.float32)
        tile_wide = tile_block.astype(jnp.float32)
        if transposed:
            products = jnp.einsum("gba,gbd->gad", tile_wide, picked, precision=lax.Precision.HIGHEST)
        else:
            products = jnp.einsum("gab,gbd->gad", tile_wide, picked, precision=lax.Precision.HIGHEST)
        onehot = (place_group[None, :] == targets[:, None]).astype(jnp.float32)
        return running + jnp.einsum("og,gad->oad", onehot, products, precision=lax.Precision.HIGHEST), None

    start_value = jnp.zeros((out_blocks, tile_size, feat_width), jnp.float32)
    running, _ = lax.scan(advance, start_value, (grouped, picks, places))
    return running


def reference(features, w_self, w_neigh, local_tiles, local_rows, local_cols, halo_tiles, halo_rows, halo_cols, cut_rows, cut_counts, cotangent):
    nodes_x = features.reshape(N_DOM, N_REP, R, D)
    cot_all = cotangent.reshape(N_DOM, N_REP, R, D)
    ltiles = local_tiles.reshape(N_DOM, N_REP, NL, TB, TB)
    lrows = local_rows.reshape(N_DOM, N_REP, NL)
    lcols = local_cols.reshape(N_DOM, N_REP, NL)
    htiles = halo_tiles.reshape(N_DOM, N_REP, NH, TB, TB)
    hrows = halo_rows.reshape(N_DOM, N_REP, NH)
    hcols = halo_cols.reshape(N_DOM, N_REP, NH)
    slot_index = jnp.arange(C, dtype=jnp.int32)
    live_slots = slot_index[None, None, None, :] < cut_counts[..., None]
    grad_scale = float(NODES) ** -0.5
    senders = jnp.arange(N_DOM, dtype=jnp.int32)

    def partition(carry, part_index):
        dx_halo, sum_self, sum_neigh = carry
        part_blocks = nodes_x[part_index].reshape(PB, TB, D)
        back_part = jnp.zeros((PB, TB, D), jnp.float32)
        out_rows = []
        rest_rows = []
        for rep_index in range(N_REP):
            cut_list = cut_rows[:, rep_index, part_index, :]
            gathered = jax.vmap(lambda block, idx: jnp.take(block, idx, axis=0))(nodes_x[:, rep_index], cut_list)
            live_here = live_slots[:, rep_index, part_index, :]
            incoming = jnp.where(live_here[:, :, None], gathered, jnp.zeros_like(gathered)).astype(jnp.bfloat16)
            halo_blocks = incoming.reshape(HB, TB, D)
            own_x = nodes_x[part_index, rep_index]
            summed = aggregate(part_blocks, ltiles[part_index, rep_index], lcols[part_index, rep_index], lrows[part_index, rep_index], RB, False)
            summed = summed + aggregate(halo_blocks, htiles[part_index, rep_index], hcols[part_index, rep_index], hrows[part_index, rep_index], RB, False)
            neighbour = summed.reshape(R, D).astype(jnp.bfloat16)
            preact = jnp.dot(own_x, w_self, preferred_element_type=jnp.float32) + jnp.dot(neighbour, w_neigh, preferred_element_type=jnp.float32)
            sigmoid_pre = jax.nn.sigmoid(preact)
            out_rows.append((preact * sigmoid_pre).astype(jnp.bfloat16))
            slope_value = sigmoid_pre * (1.0 + preact * (1.0 - sigmoid_pre))
            grad_pre = (cot_all[part_index, rep_index].astype(jnp.float32) * slope_value).astype(jnp.bfloat16)
            sum_self = sum_self + lax.dot_general(own_x, grad_pre, (((0,), (0,)), ((), ())), preferred_element_type=jnp.float32)
            sum_neigh = sum_neigh + lax.dot_general(neighbour, grad_pre, (((0,), (0,)), ((), ())), preferred_element_type=jnp.float32)
            grad_agg = jnp.dot(grad_pre, w_neigh.T, preferred_element_type=jnp.float32).astype(jnp.bfloat16)
            grad_self = jnp.dot(grad_pre, w_self.T, preferred_element_type=jnp.float32)
            agg_blocks = grad_agg.reshape(RB, TB, D)
            term = aggregate(agg_blocks, ltiles[part_index, rep_index], lrows[part_index, rep_index], lcols[part_index, rep_index], PB, True)
            back_part = back_part + lax.optimization_barrier(term.astype(jnp.bfloat16)).astype(jnp.float32)
            halo_back = aggregate(agg_blocks, htiles[part_index, rep_index], hrows[part_index, rep_index], hcols[part_index, rep_index], HB, True)
            halo_back = halo_back.astype(jnp.bfloat16).reshape(N_DOM, C, D).astype(jnp.float32)
            masked = jnp.where(live_here[:, :, None], halo_back, jnp.zeros_like(halo_back))
            dx_halo = dx_halo.at[senders[:, None], rep_index, cut_list].add(masked)
            rest_rows.append(grad_self)
        rest = jnp.stack(rest_rows) + back_part.reshape(N_REP, R, D)
        return (dx_halo, sum_self, sum_neigh), (jnp.stack(out_rows), rest)

    start_carry = (jnp.zeros((N_DOM, N_REP, R, D), jnp.float32), jnp.zeros((D, D), jnp.float32), jnp.zeros((D, D), jnp.float32))
    final_carry, stacked = lax.scan(partition, start_carry, jnp.arange(N_DOM, dtype=jnp.int32))
    dx_halo, sum_self, sum_neigh = final_carry
    out_all, rest_all = stacked
    out = out_all.reshape(NODES, D)
    d_x = (rest_all + dx_halo).astype(jnp.bfloat16).reshape(NODES, D)
    return out, d_x, sum_self * grad_scale, sum_neigh * grad_scale
```

```python
import functools

import jax
import jax.numpy as jnp
from jax import lax
from jax.experimental import pallas as pl
from jax.experimental.pallas import tpu as pltpu
from jax.sharding import PartitionSpec as P


CHUNKS = 2


def densify_kernel(
    local_rows, local_cols, halo_rows, halo_cols, local_ref, halo_ref, dense_ref, hdense_ref, acc, hacc
):
    tile_size = local_ref.shape[1]

    def place(rows, cols, tiles, total):
        total[...] = jnp.zeros_like(total)

        def step(k, carry):
            row = pl.multiple_of(rows[k] * tile_size, tile_size)
            col = pl.multiple_of(cols[k] * tile_size, tile_size)
            total[pl.ds(row, tile_size), pl.ds(col, tile_size)] += tiles[k].astype(jnp.float32)
            return carry

        lax.fori_loop(0, tiles.shape[0], step, 0)

    place(local_rows, local_cols, local_ref, acc)
    dense_ref[...] = acc[...].astype(dense_ref.dtype)
    place(halo_rows, halo_cols, halo_ref, hacc)
    hdense_ref[...] = hacc[...].astype(hdense_ref.dtype)


def densify(local_tiles, local_rows, local_cols, halo_tiles, halo_rows, halo_cols, rows, cols, hcols):
    smem = pl.BlockSpec(memory_space=pltpu.SMEM)
    vmem = pl.BlockSpec(memory_space=pltpu.VMEM)
    return pl.pallas_call(
        densify_kernel,
        out_shape=(
            jax.ShapeDtypeStruct((rows, cols), jnp.bfloat16),
            jax.ShapeDtypeStruct((rows, hcols), jnp.bfloat16),
        ),
        in_specs=[smem] * 4 + [vmem] * 2,
        out_specs=(vmem, vmem),
        scratch_shapes=[pltpu.VMEM((rows, cols), jnp.float32), pltpu.VMEM((rows, hcols), jnp.float32)],
        compiler_params=pltpu.CompilerParams(vmem_limit_bytes=60 << 20),
        cost_estimate=pl.CostEstimate(
            flops=rows * cols * 2, bytes_accessed=rows * (cols + hcols) * 4, transcendentals=0
        ),
        name="densify",
    )(local_rows, local_cols, halo_rows, halo_cols, local_tiles, halo_tiles)


def dot(a, b):
    return jnp.dot(a, b, preferred_element_type=jnp.float32)


def dot_t(a, b):
    return lax.dot_general(a, b, (((0,), (0,)), ((), ())), preferred_element_type=jnp.float32)


def per_device(
    features,
    w_self,
    w_neigh,
    local_tiles,
    local_rows,
    local_cols,
    halo_tiles,
    halo_rows,
    halo_cols,
    cut_rows,
    cut_counts,
    cotangent,
):
    row_count, width = features.shape
    tile_size = local_tiles.shape[1]
    n = lax.axis_size("rep")
    dom = lax.axis_size("dom")
    me = lax.axis_index("rep")
    blocks = row_count // tile_size
    piece = row_count // CHUNKS
    paired = (n - 1) // 2
    slots = 1 + 2 * paired + (n - 1 - paired)

    offset = local_cols // blocks - me
    away = jnp.abs(offset)
    near = 2 * away - 1 + (offset < 0)
    slot = jnp.where(away == 0, 0, jnp.where(away <= paired, near, away + paired))
    slot_cols = slot * blocks + local_cols % blocks
    cut_list = cut_rows[0, 0]
    halo_size = cut_list.shape[0] * cut_list.shape[1]
    dense, hdense = densify(
        local_tiles,
        local_rows,
        slot_cols,
        halo_tiles,
        halo_rows,
        halo_cols,
        row_count,
        slots * row_count,
        halo_size,
    )

    def part(slot_id, c):
        start = slot_id * row_count + c * piece
        return dense[:, start : start + piece]

    def one_slot(k):
        return k + paired

    slot_index = jnp.arange(cut_list.shape[1], dtype=jnp.int32)
    live = slot_index[None, :] < cut_counts[0, 0][:, None]
    node_ids = jnp.arange(row_count, dtype=jnp.int32)
    selector = (
        (cut_list.reshape(-1)[:, None] == node_ids[None, :]) & live.reshape(-1)[:, None]
    ).astype(jnp.bfloat16)
    chosen = dot(selector, features).astype(jnp.bfloat16)
    incoming = lax.all_to_all(
        chosen.reshape(dom, -1, width), "dom", split_axis=0, concat_axis=0, tiled=True
    ).reshape(halo_size, width)

    def to_right(value, first, last):
        return lax.ppermute(value, "rep", [(i, i + 1) for i in range(first, last)])

    def to_left(value, first, last):
        return lax.ppermute(value, "rep", [(i + 1, i) for i in range(first, last)])

    pieces = [features[c * piece : (c + 1) * piece] for c in range(CHUNKS)]
    from_left = list(pieces)
    from_right = list(pieces)
    arrivals = []
    for k in range(1, n):
        for c in range(CHUNKS):
            from_left[c] = to_right(from_left[c], k - 1, n - 1)
            from_right[c] = to_left(from_right[c], 0, n - k)
            if k <= paired:
                arrivals.append((2 * k - 1, c, from_right[c]))
                arrivals.append((2 * k, c, from_left[c]))
            else:
                arrivals.append((one_slot(k), c, from_left[c] + from_right[c]))

    pre_self = dot(features, w_self)
    summed = dot(dense[:, :row_count], features)
    summed = summed + dot(hdense, incoming)
    for slot_id, c, rows in arrivals:
        summed = summed + dot(part(slot_id, c), rows)
    neighbour = summed.astype(jnp.bfloat16)
    preact = pre_self + dot(neighbour, w_neigh)
    sigmoid_pre = jax.nn.sigmoid(preact)
    out = (preact * sigmoid_pre).astype(jnp.bfloat16)
    slope = sigmoid_pre * (1.0 + preact * (1.0 - sigmoid_pre))
    grad_pre = (cotangent.astype(jnp.float32) * slope).astype(jnp.bfloat16)
    grad_agg = dot(grad_pre, w_neigh.T).astype(jnp.bfloat16)

    zero = [None] * CHUNKS
    sum_right, sum_left = list(zero), list(zero)

    def plus(a, *more):
        for b in more:
            if b is not None:
                a = a + b.astype(jnp.float32)
        return a.astype(jnp.bfloat16)

    for k in range(n - 1, 0, -1):
        for c in range(CHUNKS):
            if k <= paired:
                right = plus(dot_t(part(2 * k - 1, c), grad_agg), sum_right[c])
                left = plus(dot_t(part(2 * k, c), grad_agg), sum_left[c])
            else:
                right = plus(dot_t(part(one_slot(k), c), grad_agg), sum_right[c], sum_left[c])
                left = right
            sum_right[c] = to_right(right, 0, n - k)
            sum_left[c] = to_left(left, k - 1, n - 1)

    halo_back = dot_t(hdense, grad_agg).astype(jnp.bfloat16)
    returned = lax.all_to_all(
        halo_back.reshape(dom, -1, width), "dom", split_axis=0, concat_axis=0, tiled=True
    ).reshape(halo_size, width)

    grad_scale = float(row_count * n * dom) ** (-0.5)
    d_self = (dot_t(features, grad_pre) * grad_scale).astype(jnp.bfloat16)
    d_neigh = (dot_t(neighbour, grad_pre) * grad_scale).astype(jnp.bfloat16)
    share = width // (n * dom)
    both = jnp.stack([d_self, d_neigh]).reshape(2, n, dom, share, width)
    both = jnp.transpose(both, (2, 1, 0, 3, 4))
    both = lax.all_to_all(both, "dom", split_axis=0, concat_axis=0, tiled=True)
    both = jnp.sum(both.astype(jnp.float32), axis=0)
    both = lax.all_to_all(both, "rep", split_axis=0, concat_axis=0, tiled=True)
    both = jnp.sum(both, axis=0)
    both = lax.all_to_all(
        jnp.broadcast_to(both[None], (dom, 2, share, width)),
        "dom",
        split_axis=0,
        concat_axis=0,
        tiled=True,
    )
    d_w_self = both[:, 0].reshape(width // n, width)
    d_w_neigh = both[:, 1].reshape(width // n, width)

    d_x = dot(grad_pre, w_self.T) + dot_t(dense[:, :row_count], grad_agg)
    d_x = d_x + dot_t(selector, returned)
    far = jnp.concatenate([a.astype(jnp.float32) + b.astype(jnp.float32) for a, b in zip(sum_right, sum_left)])
    d_x = (d_x + far).astype(jnp.bfloat16)
    return (out, d_x, d_w_self, d_w_neigh)


def solution(mesh):
    lead = ("dom", "rep")
    in_specs = (
        P(lead, None),
        P(),
        P(),
        P(lead, None, None),
        P(lead),
        P(lead),
        P(lead, None, None),
        P(lead),
        P(lead),
        P("dom", "rep", None, None),
        P("dom", "rep", None),
        P(lead, None),
    )
    out_specs = (P(lead, None), P(lead, None), P("rep", None), P("rep", None))
    return jax.shard_map(
        per_device, mesh=mesh, in_specs=in_specs, out_specs=out_specs, check_vma=False
    )
```

```python
import math

import jax
import jax.numpy as jnp
from jax import lax
from jax.experimental import pallas as pl
from jax.experimental.pallas import tpu as pltpu
from jax.sharding import PartitionSpec as P


ROW_STEP = 256


def densify_kernel(
    local_rows, local_cols, halo_rows, halo_cols, local_ref, halo_ref, dense_ref, hdense_ref, acc, hacc
):
    tile_size = local_ref.shape[1]

    def place(rows, cols, tiles, total):
        total[...] = jnp.zeros_like(total)

        def step(k, carry):
            row = pl.multiple_of(rows[k] * tile_size, tile_size)
            col = pl.multiple_of(cols[k] * tile_size, tile_size)
            total[pl.ds(row, tile_size), pl.ds(col, tile_size)] += tiles[k].astype(jnp.float32)
            return carry

        lax.fori_loop(0, tiles.shape[0], step, 0)

    place(local_rows, local_cols, local_ref, acc)
    dense_ref[...] = acc[...].astype(dense_ref.dtype)
    place(halo_rows, halo_cols, halo_ref, hacc)
    hdense_ref[...] = hacc[...].astype(hdense_ref.dtype)


def densify(local_tiles, local_rows, local_cols, halo_tiles, halo_rows, halo_cols, rows, cols, hcols):
    smem = pl.BlockSpec(memory_space=pltpu.SMEM)
    vmem = pl.BlockSpec(memory_space=pltpu.VMEM)
    return pl.pallas_call(
        densify_kernel,
        out_shape=(
            jax.ShapeDtypeStruct((rows, cols), jnp.bfloat16),
            jax.ShapeDtypeStruct((rows, hcols), jnp.bfloat16),
        ),
        in_specs=[smem] * 4 + [vmem] * 2,
        out_specs=(vmem, vmem),
        scratch_shapes=[pltpu.VMEM((rows, cols), jnp.float32), pltpu.VMEM((rows, hcols), jnp.float32)],
        compiler_params=pltpu.CompilerParams(vmem_limit_bytes=60 << 20),
        cost_estimate=pl.CostEstimate(
            flops=rows * cols * 2, bytes_accessed=rows * (cols + hcols) * 4, transcendentals=0
        ),
        name="densify",
    )(local_rows, local_cols, halo_rows, halo_cols, local_tiles, halo_tiles)


def dot(a, b):
    return jnp.dot(a, b, preferred_element_type=jnp.float32)


def dot_t(a, b):
    return lax.dot_general(a, b, (((0,), (0,)), ((), ())), preferred_element_type=jnp.float32)


def middle_kernel(
    acc_ref, dense_ref, outer_ref, inner_ref, pre_ref, cot_ref, w_ref,
    out_ref, neighbour_ref, grad_ref, agg_ref, term_ref, total, far,
):
    step = pl.program_id(0)

    @pl.when(step == 0)
    def _():
        far[...] = outer_ref[...] + inner_ref[...]

    dense = dense_ref[...]
    neighbour = (acc_ref[...] + dot(dense, far[...])).astype(jnp.bfloat16)
    neighbour_ref[...] = neighbour
    preact = pre_ref[...] + dot(neighbour, w_ref[...])
    sigmoid_pre = jax.nn.sigmoid(preact)
    out_ref[...] = (preact * sigmoid_pre).astype(out_ref.dtype)
    slope = sigmoid_pre * (1.0 + preact * (1.0 - sigmoid_pre))
    grad = (cot_ref[...].astype(jnp.float32) * slope).astype(jnp.bfloat16)
    grad_ref[...] = grad
    agg = lax.dot_general(
        grad, w_ref[...], (((1,), (1,)), ((), ())), preferred_element_type=jnp.float32
    ).astype(jnp.bfloat16)
    agg_ref[...] = agg
    term = dot_t(dense, agg)

    @pl.when(step == 0)
    def _():
        total[...] = term

    @pl.when(step > 0)
    def _():
        total[...] += term

    @pl.when(step == pl.num_programs(0) - 1)
    def _():
        term_ref[...] = total[...].astype(term_ref.dtype)


def middle(acc, dense, slot, outer, inner, pre_self, cotangent, w_neigh):
    rows, width = acc.shape
    step = math.gcd(rows, ROW_STEP)
    by_rows = pl.BlockSpec((step, width), lambda i: (i, 0))
    like = jax.ShapeDtypeStruct((rows, width), jnp.bfloat16)
    return pl.pallas_call(
        middle_kernel,
        grid=(rows // step,),
        out_shape=(like,) * 5,
        in_specs=[
            by_rows,
            pl.BlockSpec((step, rows), lambda i: (i, slot)),
            pl.BlockSpec((rows, width), lambda i: (0, 0)),
            pl.BlockSpec((rows, width), lambda i: (0, 0)),
            by_rows,
            by_rows,
            pl.BlockSpec(w_neigh.shape, lambda i: (0, 0)),
        ],
        out_specs=(by_rows,) * 4 + (pl.BlockSpec((rows, width), lambda i: (0, 0)),),
        scratch_shapes=[pltpu.VMEM((rows, width), jnp.float32), pltpu.VMEM((rows, width), jnp.bfloat16)],
        compiler_params=pltpu.CompilerParams(vmem_limit_bytes=40 << 20),
        cost_estimate=pl.CostEstimate(
            flops=4 * rows * width * (rows + width), bytes_accessed=18 << 20, transcendentals=rows * width
        ),
        name="middle",
    )(acc, dense, outer, inner, pre_self, cotangent, w_neigh)


def per_device(
    features,
    w_self,
    w_neigh,
    local_tiles,
    local_rows,
    local_cols,
    halo_tiles,
    halo_rows,
    halo_cols,
    cut_rows,
    cut_counts,
    cotangent,
):
    row_count, width = features.shape
    tile_size = local_tiles.shape[1]
    n = lax.axis_size("rep")
    dom = lax.axis_size("dom")
    me = lax.axis_index("rep")
    blocks = row_count // tile_size
    assert n == 4
    swap_one = [(0, 1), (1, 0), (2, 3), (3, 2)]
    swap_two = [(0, 2), (1, 3), (2, 0), (3, 1)]
    swap_inner = [(1, 2), (2, 1)]
    outward, inward = [(1, 0), (2, 3)], [(0, 1), (3, 2)]

    def move(value, pairs):
        return lax.ppermute(value, "rep", pairs)

    second = move(features, swap_two)
    first = move(features, swap_one)
    inner = move(features, swap_inner)

    slot = jnp.bitwise_xor(local_cols // blocks, me)
    slot_cols = slot * blocks + local_cols % blocks
    cut_list = cut_rows[0, 0]
    halo_size = cut_list.shape[0] * cut_list.shape[1]
    dense, hdense = densify(
        local_tiles,
        local_rows,
        slot_cols,
        halo_tiles,
        halo_rows,
        halo_cols,
        row_count,
        n * row_count,
        halo_size,
    )

    def part(slot_id):
        return dense[:, slot_id * row_count : (slot_id + 1) * row_count]

    slot_index = jnp.arange(cut_list.shape[1], dtype=jnp.int32)
    live = slot_index[None, :] < cut_counts[0, 0][:, None]
    node_ids = jnp.arange(row_count, dtype=jnp.int32)
    selector = (
        (cut_list.reshape(-1)[:, None] == node_ids[None, :]) & live.reshape(-1)[:, None]
    ).astype(jnp.bfloat16)
    chosen = dot(selector, features).astype(jnp.bfloat16)
    incoming = lax.all_to_all(
        chosen.reshape(dom, -1, width), "dom", split_axis=0, concat_axis=0, tiled=True
    ).reshape(halo_size, width)

    pre_self = dot(features, w_self)
    summed = dot(part(0), features) + dot(hdense, incoming)
    third = move(second, outward)
    summed = summed + dot(part(1), first)
    summed = summed + dot(part(2), second)
    out, neighbour, grad_pre, grad_agg, term = middle(
        summed, dense, 3, third, inner, pre_self, cotangent, w_neigh
    )

    passed = move(term, inward)
    near = move(term, swap_inner)

    grad_scale = float(row_count * n * dom) ** (-0.5)
    share = width // (n * dom)
    d_self = (dot_t(features, grad_pre) * grad_scale).astype(jnp.bfloat16)
    d_neigh = (dot_t(neighbour, grad_pre) * grad_scale).astype(jnp.bfloat16)
    halo_back = dot_t(hdense, grad_agg).astype(jnp.bfloat16)
    both = jnp.stack([d_self, d_neigh]).reshape(2, n, dom, share, width)
    both = jnp.transpose(both, (2, 1, 0, 3, 4)).reshape(dom, 2 * n * share, width)
    both = jnp.concatenate([halo_back.reshape(dom, -1, width), both], axis=1)
    both = lax.all_to_all(both, "dom", split_axis=0, concat_axis=0, tiled=True)
    slots = cut_list.shape[1]
    returned = both[:, :slots].reshape(halo_size, width)
    both = jnp.sum(both[:, slots:].astype(jnp.float32), axis=0).reshape(n, 2, share, width)
    both = lax.all_to_all(both, "rep", split_axis=0, concat_axis=0, tiled=True)
    both = jnp.sum(both, axis=0)
    both = lax.all_to_all(
        jnp.broadcast_to(both[None], (dom, 2, share, width)),
        "dom",
        split_axis=0,
        concat_axis=0,
        tiled=True,
    )
    d_w_self = both[:, 0].reshape(width // n, width)
    d_w_neigh = both[:, 1].reshape(width // n, width)

    one_term = dot_t(part(1), grad_agg).astype(jnp.bfloat16)
    one = move(one_term, swap_one)
    two_term = lax.optimization_barrier(dot_t(part(2), grad_agg))
    two_term = (two_term + passed.astype(jnp.float32)).astype(jnp.bfloat16)
    half = row_count // 2
    two_a = move(two_term[:half], swap_two)
    two_b = move(two_term[half:], swap_two)

    d_x = dot(grad_pre, w_self.T) + dot_t(part(0), grad_agg)
    d_x = d_x + dot_t(selector, returned)
    d_x = d_x + near.astype(jnp.float32) + one.astype(jnp.float32)
    d_x = lax.optimization_barrier(d_x)
    d_x = jnp.concatenate(
        [
            (d_x[:half] + two_a.astype(jnp.float32)).astype(jnp.bfloat16),
            (d_x[half:] + two_b.astype(jnp.float32)).astype(jnp.bfloat16),
        ]
    )
    return (out, d_x, d_w_self, d_w_neigh)


def solution(mesh):
    lead = ("dom", "rep")
    in_specs = (
        P(lead, None),
        P(),
        P(),
        P(lead, None, None),
        P(lead),
        P(lead),
        P(lead, None, None),
        P(lead),
        P(lead),
        P("dom", "rep", None, None),
        P("dom", "rep", None),
        P(lead, None),
    )
    out_specs = (P(lead, None), P(lead, None), P("rep", None), P("rep", None))

    return jax.shard_map(per_device, mesh=mesh, in_specs=in_specs, out_specs=out_specs, check_vma=False)
```

```python
import math

import jax
import jax.numpy as jnp
from jax import lax
from jax.experimental import pallas as pl
from jax.experimental.pallas import tpu as pltpu
from jax.sharding import PartitionSpec as P


ROW_STEP = 256


def densify_kernel(
    local_rows, local_cols, halo_rows, halo_cols, local_ref, halo_ref, dense_ref, hdense_ref, acc, hacc
):
    tile_size = local_ref.shape[1]

    def place(rows, cols, tiles, total):
        total[...] = jnp.zeros_like(total)

        def step(k, carry):
            row = pl.multiple_of(rows[k] * tile_size, tile_size)
            col = pl.multiple_of(cols[k] * tile_size, tile_size)
            total[pl.ds(row, tile_size), pl.ds(col, tile_size)] += tiles[k].astype(jnp.float32)
            return carry

        lax.fori_loop(0, tiles.shape[0], step, 0)

    place(local_rows, local_cols, local_ref, acc)
    dense_ref[...] = acc[...].astype(dense_ref.dtype)
    place(halo_rows, halo_cols, halo_ref, hacc)
    hdense_ref[...] = hacc[...].astype(hdense_ref.dtype)


def densify(local_tiles, local_rows, local_cols, halo_tiles, halo_rows, halo_cols, rows, cols, hcols):
    smem = pl.BlockSpec(memory_space=pltpu.SMEM)
    vmem = pl.BlockSpec(memory_space=pltpu.VMEM)
    return pl.pallas_call(
        densify_kernel,
        out_shape=(
            jax.ShapeDtypeStruct((rows, cols), jnp.bfloat16),
            jax.ShapeDtypeStruct((rows, hcols), jnp.bfloat16),
        ),
        in_specs=[smem] * 4 + [vmem] * 2,
        out_specs=(vmem, vmem),
        scratch_shapes=[pltpu.VMEM((rows, cols), jnp.float32), pltpu.VMEM((rows, hcols), jnp.float32)],
        compiler_params=pltpu.CompilerParams(vmem_limit_bytes=60 << 20),
        cost_estimate=pl.CostEstimate(
            flops=rows * cols * 2, bytes_accessed=rows * (cols + hcols) * 4, transcendentals=0
        ),
        name="densify",
    )(local_rows, local_cols, halo_rows, halo_cols, local_tiles, halo_tiles)


def dot(a, b):
    return jnp.dot(a, b, preferred_element_type=jnp.float32)


def dot_t(a, b):
    return lax.dot_general(a, b, (((0,), (0,)), ((), ())), preferred_element_type=jnp.float32)


def middle_kernel(
    acc_ref, dense_ref, outer_ref, inner_ref, pre_ref, cot_ref, w_ref,
    out_ref, neighbour_ref, grad_ref, agg_ref, term_ref, total, far,
):
    step = pl.program_id(0)
    half = far.shape[0]

    @pl.when(step == 0)
    def _():
        far[...] = outer_ref[...] + inner_ref[...]

    dense = dense_ref[...]
    neighbour = (acc_ref[...] + dot(dense[:, -half:], far[...])).astype(jnp.bfloat16)
    neighbour_ref[...] = neighbour
    preact = pre_ref[...] + dot(neighbour, w_ref[...])
    sigmoid_pre = jax.nn.sigmoid(preact)
    out_ref[...] = (preact * sigmoid_pre).astype(out_ref.dtype)
    slope = sigmoid_pre * (1.0 + preact * (1.0 - sigmoid_pre))
    grad = (cot_ref[...].astype(jnp.float32) * slope).astype(jnp.bfloat16)
    grad_ref[...] = grad
    agg = lax.dot_general(
        grad, w_ref[...], (((1,), (1,)), ((), ())), preferred_element_type=jnp.float32
    ).astype(jnp.bfloat16)
    agg_ref[...] = agg
    term = dot_t(dense, agg)

    @pl.when(step == 0)
    def _():
        total[...] = term

    @pl.when(step > 0)
    def _():
        total[...] += term

    @pl.when(step == pl.num_programs(0) - 1)
    def _():
        term_ref[...] = total[...].astype(term_ref.dtype)


def middle(acc, dense, slot, outer, inner, pre_self, cotangent, w_neigh):
    rows, width = acc.shape
    step = math.gcd(rows, ROW_STEP)
    by_rows = pl.BlockSpec((step, width), lambda i: (i, 0))
    like = jax.ShapeDtypeStruct((rows, width), jnp.bfloat16)
    return pl.pallas_call(
        middle_kernel,
        grid=(rows // step,),
        out_shape=(like,) * 5,
        in_specs=[
            by_rows,
            pl.BlockSpec((step, rows), lambda i: (i, slot)),
            pl.BlockSpec(outer.shape, lambda i: (0, 0)),
            pl.BlockSpec(outer.shape, lambda i: (0, 0)),
            by_rows,
            by_rows,
            pl.BlockSpec(w_neigh.shape, lambda i: (0, 0)),
        ],
        out_specs=(by_rows,) * 4 + (pl.BlockSpec((rows, width), lambda i: (0, 0)),),
        scratch_shapes=[pltpu.VMEM((rows, width), jnp.float32), pltpu.VMEM(outer.shape, jnp.bfloat16)],
        compiler_params=pltpu.CompilerParams(vmem_limit_bytes=40 << 20),
        cost_estimate=pl.CostEstimate(
            flops=4 * rows * width * (rows + width), bytes_accessed=18 << 20, transcendentals=rows * width
        ),
        name="middle",
    )(acc, dense, outer, inner, pre_self, cotangent, w_neigh)


def per_device(
    features,
    w_self,
    w_neigh,
    local_tiles,
    local_rows,
    local_cols,
    halo_tiles,
    halo_rows,
    halo_cols,
    cut_rows,
    cut_counts,
    cotangent,
):
    row_count, width = features.shape
    tile_size = local_tiles.shape[1]
    n = lax.axis_size("rep")
    dom = lax.axis_size("dom")
    me = lax.axis_index("rep")
    blocks = row_count // tile_size
    assert n == 4
    first_out = [(0, 1), (3, 2), (1, 3), (2, 0)]
    second_out = [(0, 2), (3, 1), (1, 0), (2, 3)]
    first_in = [(b, a) for a, b in first_out]
    second_in = [(b, a) for a, b in second_out]
    swap_inner = [(1, 2), (2, 1)]
    outward, inward = [(1, 0), (2, 3)], [(0, 1), (3, 2)]

    def move(value, pairs):
        return lax.ppermute(value, "rep", pairs)

    half = row_count // 2
    low, high = features[:half], features[half:]
    second = move(features, second_in)
    first_a = move(low, first_in)
    first_b = move(high, first_in)
    inner_a, inner_b = move(low, swap_inner), move(high, swap_inner)

    slot = jnp.bitwise_xor(local_cols // blocks, me)
    crossed = ((me == 1) | (me == 2)) & ((slot == 1) | (slot == 2))
    slot = jnp.where(crossed, 3 - slot, slot)
    slot_cols = slot * blocks + local_cols % blocks
    cut_list = cut_rows[0, 0]
    halo_size = cut_list.shape[0] * cut_list.shape[1]
    dense, hdense = densify(
        local_tiles,
        local_rows,
        slot_cols,
        halo_tiles,
        halo_rows,
        halo_cols,
        row_count,
        n * row_count,
        halo_size,
    )

    def part(slot_id):
        return dense[:, slot_id * row_count : (slot_id + 1) * row_count]

    slot_index = jnp.arange(cut_list.shape[1], dtype=jnp.int32)
    live = slot_index[None, :] < cut_counts[0, 0][:, None]
    node_ids = jnp.arange(row_count, dtype=jnp.int32)
    selector = (
        (cut_list.reshape(-1)[:, None] == node_ids[None, :]) & live.reshape(-1)[:, None]
    ).astype(jnp.bfloat16)
    chosen = dot(selector, features).astype(jnp.bfloat16)
    incoming = lax.all_to_all(
        chosen.reshape(dom, -1, width), "dom", split_axis=0, concat_axis=0, tiled=True
    ).reshape(halo_size, width)

    pre_self = dot(features, w_self)
    summed = dot(part(0), features) + dot(hdense, incoming)
    third_a = move(first_a, outward)
    third_b = move(first_b, outward)
    summed = summed + dot(part(2), second)
    summed = summed + dot(part(1)[:, :half], first_a) + dot(part(1)[:, half:], first_b)
    summed = lax.optimization_barrier(summed)
    summed = summed + dot(part(3)[:, :half], third_a + inner_a)
    out, neighbour, grad_pre, grad_agg, term = middle(
        summed, dense, 3, third_b, inner_b, pre_self, cotangent, w_neigh
    )

    passed = move(term, inward)
    near = move(term, swap_inner)

    grad_scale = float(row_count * n * dom) ** (-0.5)
    share = width // (n * dom)
    d_self = (dot_t(features, grad_pre) * grad_scale).astype(jnp.bfloat16)
    d_neigh = (dot_t(neighbour, grad_pre) * grad_scale).astype(jnp.bfloat16)
    halo_back = dot_t(hdense, grad_agg).astype(jnp.bfloat16)
    both = jnp.stack([d_self, d_neigh]).reshape(2, n, dom, share, width)
    both = jnp.transpose(both, (2, 1, 0, 3, 4)).reshape(dom, 2 * n * share, width)
    both = jnp.concatenate([halo_back.reshape(dom, -1, width), both], axis=1)
    both = lax.all_to_all(both, "dom", split_axis=0, concat_axis=0, tiled=True)
    slots = cut_list.shape[1]
    returned = both[:, :slots].reshape(halo_size, width)
    both = jnp.sum(both[:, slots:].astype(jnp.float32), axis=0).reshape(n, 2, share, width)
    both = lax.all_to_all(both, "rep", split_axis=0, concat_axis=0, tiled=True)
    both = jnp.sum(both, axis=0)
    both = jnp.broadcast_to(both[None], (dom, 2, share, width))
    both = lax.all_to_all(
        both,
        "dom",
        split_axis=0,
        concat_axis=0,
        tiled=True,
    )
    d_w_self = both[:, 0].reshape(width // n, width)
    d_w_neigh = both[:, 1].reshape(width // n, width)

    second_term = dot_t(part(2), grad_agg).astype(jnp.bfloat16)
    second_back = move(second_term, second_out)
    first_term = lax.optimization_barrier(dot_t(part(1), grad_agg))
    first_term = first_term + passed.astype(jnp.float32)
    last_a = move(first_term[:half].astype(jnp.bfloat16), first_out)
    last_b = move(first_term[half:].astype(jnp.bfloat16), first_out)

    d_x = dot(grad_pre, w_self.T) + dot_t(part(0), grad_agg)
    d_x = d_x + dot_t(selector, returned)
    d_x = d_x + near.astype(jnp.float32)
    d_x = d_x + second_back.astype(jnp.float32)
    d_x = lax.optimization_barrier(d_x)
    base = jnp.concatenate([last_a.astype(jnp.float32), jnp.zeros((row_count - half, width))])
    base = lax.optimization_barrier((d_x + base).astype(jnp.bfloat16))
    last = (d_x[half:] + last_b.astype(jnp.float32)).astype(jnp.bfloat16)
    d_x = lax.dynamic_update_slice_in_dim(base, last, half, 0)
    return (out, d_x, d_w_self, d_w_neigh)


def solution(mesh):
    lead = ("dom", "rep")
    in_specs = (
        P(lead, None),
        P(),
        P(),
        P(lead, None, None),
        P(lead),
        P(lead),
        P(lead, None, None),
        P(lead),
        P(lead),
        P("dom", "rep", None, None),
        P("dom", "rep", None),
        P(lead, None),
    )
    out_specs = (P(lead, None), P(lead, None), P("rep", None), P("rep", None))

    return jax.shard_map(per_device, mesh=mesh, in_specs=in_specs, out_specs=out_specs, check_vma=False)
```

```python
import math

import jax
import jax.numpy as jnp
from jax import lax
from jax.experimental import pallas as pl
from jax.experimental.pallas import tpu as pltpu
from jax.sharding import PartitionSpec as P


ROW_STEP = 512


def densify_kernel(
    local_rows, local_cols, halo_rows, halo_cols, local_ref, halo_ref, *refs
):
    *dense_refs, hdense_ref, acc, hacc = refs
    tile_size = local_ref.shape[1]

    def place(rows, cols, tiles, total):
        total[...] = jnp.zeros_like(total)

        def step(k, carry):
            row = pl.multiple_of(rows[k] * tile_size, tile_size)
            col = pl.multiple_of(cols[k] * tile_size, tile_size)
            total[pl.ds(row, tile_size), pl.ds(col, tile_size)] += tiles[k].astype(jnp.float32)
            return carry

        lax.fori_loop(0, tiles.shape[0], step, 0)

    place(local_rows, local_cols, local_ref, acc)
    for i, ref in enumerate(dense_refs):
        ref[...] = acc[:, i * ref.shape[1] : (i + 1) * ref.shape[1]].astype(ref.dtype)
    place(halo_rows, halo_cols, halo_ref, hacc)
    hdense_ref[...] = hacc[...].astype(hdense_ref.dtype)


def densify(local_tiles, local_rows, local_cols, halo_tiles, halo_rows, halo_cols, rows, slots, hcols):
    smem = pl.BlockSpec(memory_space=pltpu.SMEM)
    vmem = pl.BlockSpec(memory_space=pltpu.VMEM)
    cols = rows * slots
    *parts, halo = pl.pallas_call(
        densify_kernel,
        out_shape=(jax.ShapeDtypeStruct((rows, rows), jnp.bfloat16),) * slots
        + (jax.ShapeDtypeStruct((rows, hcols), jnp.bfloat16),),
        in_specs=[smem] * 4 + [vmem] * 2,
        out_specs=(vmem,) * (slots + 1),
        scratch_shapes=[pltpu.VMEM((rows, cols), jnp.float32), pltpu.VMEM((rows, hcols), jnp.float32)],
        compiler_params=pltpu.CompilerParams(vmem_limit_bytes=60 << 20),
        cost_estimate=pl.CostEstimate(
            flops=rows * cols * 2, bytes_accessed=rows * (cols + hcols) * 4, transcendentals=0
        ),
        name="densify",
    )(local_rows, local_cols, halo_rows, halo_cols, local_tiles, halo_tiles)
    return parts, halo


def dot(a, b):
    return jnp.dot(a, b, preferred_element_type=jnp.float32)


def dot_t(a, b):
    return lax.dot_general(a, b, (((0,), (0,)), ((), ())), preferred_element_type=jnp.float32)


def middle_kernel(
    acc_ref, dense_ref, outer_ref, inner_ref, pre_ref, cot_ref, w_ref,
    out_ref, neighbour_ref, grad_ref, agg_ref, term_ref,
):
    rows, half = acc_ref.shape[0], outer_ref.shape[0]
    step = math.gcd(rows, ROW_STEP)
    far = outer_ref[...] + inner_ref[...]
    w = w_ref[...]
    for start in range(0, rows, step):
        at = slice(start, start + step)
        neighbour = acc_ref[at, :] + dot(dense_ref[at, rows - half :], far)
        neighbour = neighbour.astype(jnp.bfloat16)
        neighbour_ref[at, :] = neighbour
        preact = pre_ref[at, :] + dot(neighbour, w)
        sigmoid_pre = jax.nn.sigmoid(preact)
        out_ref[at, :] = (preact * sigmoid_pre).astype(out_ref.dtype)
        slope = sigmoid_pre * (1.0 + preact * (1.0 - sigmoid_pre))
        grad = (cot_ref[at, :].astype(jnp.float32) * slope).astype(jnp.bfloat16)
        grad_ref[at, :] = grad
        agg_ref[at, :] = lax.dot_general(
            grad, w, (((1,), (1,)), ((), ())), preferred_element_type=jnp.float32
        ).astype(jnp.bfloat16)
    for start in range(0, rows, step):
        at = slice(start, start + step)
        term_ref[at, :] = dot_t(dense_ref[:, at], agg_ref[...]).astype(term_ref.dtype)


def middle(acc, dense, outer, inner, pre_self, cotangent, w_neigh):
    rows, width = acc.shape
    vmem = pl.BlockSpec(memory_space=pltpu.VMEM)
    return pl.pallas_call(
        middle_kernel,
        out_shape=(jax.ShapeDtypeStruct((rows, width), jnp.bfloat16),) * 5,
        in_specs=[vmem] * 7,
        out_specs=(vmem,) * 5,
        compiler_params=pltpu.CompilerParams(vmem_limit_bytes=40 << 20),
        cost_estimate=pl.CostEstimate(
            flops=4 * rows * width * (rows + width), bytes_accessed=18 << 20, transcendentals=rows * width
        ),
        name="middle",
    )(acc, dense, outer, inner, pre_self, cotangent, w_neigh)


def per_device(
    features,
    w_self,
    w_neigh,
    local_tiles,
    local_rows,
    local_cols,
    halo_tiles,
    halo_rows,
    halo_cols,
    cut_rows,
    cut_counts,
    cotangent,
):
    row_count, width = features.shape
    tile_size = local_tiles.shape[1]
    n = lax.axis_size("rep")
    dom = lax.axis_size("dom")
    me = lax.axis_index("rep")
    blocks = row_count // tile_size
    assert n == 4
    first_out = [(0, 1), (3, 2), (1, 3), (2, 0)]
    second_out = [(0, 2), (3, 1), (1, 0), (2, 3)]
    first_in = [(b, a) for a, b in first_out]
    second_in = [(b, a) for a, b in second_out]
    swap_inner = [(1, 2), (2, 1)]
    outward, inward = [(1, 0), (2, 3)], [(0, 1), (3, 2)]

    def move(value, pairs):
        return lax.ppermute(value, "rep", pairs)

    half = row_count // 2
    low, high = features[:half], features[half:]
    second = move(features, second_in)
    first_a = move(low, first_in)
    first_b = move(high, first_in)
    inner_a, inner_b = move(low, swap_inner), move(high, swap_inner)

    slot = jnp.bitwise_xor(local_cols // blocks, me)
    crossed = ((me == 1) | (me == 2)) & ((slot == 1) | (slot == 2))
    slot = jnp.where(crossed, 3 - slot, slot)
    slot_cols = slot * blocks + local_cols % blocks
    cut_list = cut_rows[0, 0]
    halo_size = cut_list.shape[0] * cut_list.shape[1]
    parts, hdense = densify(
        local_tiles,
        local_rows,
        slot_cols,
        halo_tiles,
        halo_rows,
        halo_cols,
        row_count,
        n,
        halo_size,
    )

    def part(slot_id):
        return parts[slot_id]

    slot_index = jnp.arange(cut_list.shape[1], dtype=jnp.int32)
    live = slot_index[None, :] < cut_counts[0, 0][:, None]
    node_ids = jnp.arange(row_count, dtype=jnp.int32)
    selector = (
        (cut_list.reshape(-1)[:, None] == node_ids[None, :]) & live.reshape(-1)[:, None]
    ).astype(jnp.bfloat16)
    chosen = dot(selector, features).astype(jnp.bfloat16)
    incoming = lax.all_to_all(
        chosen.reshape(dom, -1, width), "dom", split_axis=0, concat_axis=0, tiled=True
    ).reshape(halo_size, width)

    pre_self = dot(features, w_self)
    summed = dot(part(0), features) + dot(hdense, incoming)
    third_a = move(first_a, outward)
    third_b = move(first_b, outward)
    summed = summed + dot(part(2), second)
    summed = summed + dot(part(1)[:, :half], first_a) + dot(part(1)[:, half:], first_b)
    summed = lax.optimization_barrier(summed)
    summed = summed + dot(part(3)[:, :half], third_a + inner_a)
    out, neighbour, grad_pre, grad_agg, term = middle(
        summed, part(3), third_b, inner_b, pre_self, cotangent, w_neigh
    )

    passed = move(term, inward)
    near = move(term, swap_inner)

    grad_scale = float(row_count * n * dom) ** (-0.5)
    share = width // (n * dom)
    d_self = (dot_t(features, grad_pre) * grad_scale).astype(jnp.bfloat16)
    d_neigh = (dot_t(neighbour, grad_pre) * grad_scale).astype(jnp.bfloat16)
    halo_back = dot_t(hdense, grad_agg).astype(jnp.bfloat16)
    both = jnp.stack([d_self, d_neigh]).reshape(2, n, dom, share, width)
    both = jnp.transpose(both, (2, 1, 0, 3, 4)).reshape(dom, 2 * n * share, width)
    both = jnp.concatenate([halo_back.reshape(dom, -1, width), both], axis=1)
    both = lax.all_to_all(both, "dom", split_axis=0, concat_axis=0, tiled=True)
    slots = cut_list.shape[1]
    returned = both[:, :slots].reshape(halo_size, width)
    both = jnp.sum(both[:, slots:].astype(jnp.float32), axis=0).reshape(n, 2, share, width)
    both = both.astype(jnp.bfloat16)
    both = lax.all_to_all(both, "rep", split_axis=0, concat_axis=0, tiled=True)
    both = jnp.sum(both.astype(jnp.float32), axis=0)
    both = jnp.broadcast_to(both[None], (dom, 2, share, width))
    both = lax.all_to_all(
        both,
        "dom",
        split_axis=0,
        concat_axis=0,
        tiled=True,
    )
    d_w_self = both[:, 0].reshape(width // n, width)
    d_w_neigh = both[:, 1].reshape(width // n, width)

    second_term = dot_t(part(2), grad_agg).astype(jnp.bfloat16)
    second_back = move(second_term, second_out)
    first_term = lax.optimization_barrier(dot_t(part(1), grad_agg))
    first_term = first_term + passed.astype(jnp.float32)
    most = row_count - row_count // 4
    last_a = move(first_term[:most].astype(jnp.bfloat16), first_out)
    last_b = move(first_term[most:].astype(jnp.bfloat16), first_out)

    d_x = dot(grad_pre, w_self.T) + dot_t(part(0), grad_agg)
    d_x = d_x + dot_t(selector, returned)
    d_x = d_x + near.astype(jnp.float32)
    d_x = d_x + second_back.astype(jnp.float32)
    d_x = lax.optimization_barrier(d_x)
    base = jnp.concatenate([last_a.astype(jnp.float32), jnp.zeros((row_count - most, width))])
    base = lax.optimization_barrier((d_x + base).astype(jnp.bfloat16))
    last = (d_x[most:] + last_b.astype(jnp.float32)).astype(jnp.bfloat16)
    d_x = lax.dynamic_update_slice_in_dim(base, last, most, 0)
    return (out, d_x, d_w_self, d_w_neigh)


def solution(mesh):
    lead = ("dom", "rep")
    in_specs = (
        P(lead, None),
        P(),
        P(),
        P(lead, None, None),
        P(lead),
        P(lead),
        P(lead, None, None),
        P(lead),
        P(lead),
        P("dom", "rep", None, None),
        P("dom", "rep", None),
        P(lead, None),
    )
    out_specs = (P(lead, None), P(lead, None), P("rep", None), P("rep", None))

    return jax.shard_map(per_device, mesh=mesh, in_specs=in_specs, out_specs=out_specs, check_vma=False)
```

```python
import math

import jax
import jax.numpy as jnp
from jax import lax
from jax.experimental import pallas as pl
from jax.experimental.pallas import tpu as pltpu
from jax.sharding import PartitionSpec as P


ROW_STEP = 512


def densify_kernel(
    local_rows, local_cols, halo_rows, halo_cols, local_ref, halo_ref, *refs
):
    *dense_refs, hdense_ref, acc, hacc = refs
    tile_size = local_ref.shape[1]

    def place(rows, cols, tiles, total):
        total[...] = jnp.zeros_like(total)

        def step(k, carry):
            row = pl.multiple_of(rows[k] * tile_size, tile_size)
            col = pl.multiple_of(cols[k] * tile_size, tile_size)
            total[pl.ds(row, tile_size), pl.ds(col, tile_size)] += tiles[k].astype(jnp.float32)
            return carry

        lax.fori_loop(0, tiles.shape[0], step, 0)

    place(local_rows, local_cols, local_ref, acc)
    for i, ref in enumerate(dense_refs):
        ref[...] = acc[:, i * ref.shape[1] : (i + 1) * ref.shape[1]].astype(ref.dtype)
    place(halo_rows, halo_cols, halo_ref, hacc)
    hdense_ref[...] = hacc[...].astype(hdense_ref.dtype)


def densify(local_tiles, local_rows, local_cols, halo_tiles, halo_rows, halo_cols, rows, slots, hcols):
    smem = pl.BlockSpec(memory_space=pltpu.SMEM)
    vmem = pl.BlockSpec(memory_space=pltpu.VMEM)
    cols = rows * slots
    *parts, halo = pl.pallas_call(
        densify_kernel,
        out_shape=(jax.ShapeDtypeStruct((rows, rows), jnp.bfloat16),) * slots
        + (jax.ShapeDtypeStruct((rows, hcols), jnp.bfloat16),),
        in_specs=[smem] * 4 + [vmem] * 2,
        out_specs=(vmem,) * (slots + 1),
        scratch_shapes=[pltpu.VMEM((rows, cols), jnp.float32), pltpu.VMEM((rows, hcols), jnp.float32)],
        compiler_params=pltpu.CompilerParams(vmem_limit_bytes=60 << 20),
        cost_estimate=pl.CostEstimate(
            flops=rows * cols * 2, bytes_accessed=rows * (cols + hcols) * 4, transcendentals=0
        ),
        name="densify",
    )(local_rows, local_cols, halo_rows, halo_cols, local_tiles, halo_tiles)
    return parts, halo


def dot(a, b):
    return jnp.dot(a, b, preferred_element_type=jnp.float32)


def dot_t(a, b):
    return lax.dot_general(a, b, (((0,), (0,)), ((), ())), preferred_element_type=jnp.float32)


def middle_kernel(
    acc_ref, dense_ref, outer_ref, inner_ref, pre_ref, cot_ref, w_ref,
    out_ref, neighbour_ref, grad_ref, agg_ref, term_ref,
):
    rows, half = acc_ref.shape[0], outer_ref.shape[0]
    step = math.gcd(rows, ROW_STEP)
    far = outer_ref[...] + inner_ref[...]
    w = w_ref[...]
    for start in range(0, rows, step):
        at = slice(start, start + step)
        neighbour = acc_ref[at, :] + dot(dense_ref[at, rows - half :], far)
        neighbour = neighbour.astype(jnp.bfloat16)
        neighbour_ref[at, :] = neighbour
        preact = pre_ref[at, :] + dot(neighbour, w)
        sigmoid_pre = jax.nn.sigmoid(preact)
        out_ref[at, :] = (preact * sigmoid_pre).astype(out_ref.dtype)
        slope = sigmoid_pre * (1.0 + preact * (1.0 - sigmoid_pre))
        grad = (cot_ref[at, :].astype(jnp.float32) * slope).astype(jnp.bfloat16)
        grad_ref[at, :] = grad
        agg_ref[at, :] = lax.dot_general(
            grad, w, (((1,), (1,)), ((), ())), preferred_element_type=jnp.float32
        ).astype(jnp.bfloat16)
    term_ref[...] = dot_t(dense_ref[:, : term_ref.shape[0]], agg_ref[...]).astype(term_ref.dtype)


def middle(acc, dense, outer, inner, pre_self, cotangent, w_neigh):
    rows, width = acc.shape
    vmem = pl.BlockSpec(memory_space=pltpu.VMEM)
    return pl.pallas_call(
        middle_kernel,
        out_shape=(jax.ShapeDtypeStruct((rows, width), jnp.bfloat16),) * 4
        + (jax.ShapeDtypeStruct((rows // 2, width), jnp.bfloat16),),
        in_specs=[vmem] * 7,
        out_specs=(vmem,) * 5,
        compiler_params=pltpu.CompilerParams(vmem_limit_bytes=40 << 20),
        cost_estimate=pl.CostEstimate(
            flops=2 * rows * width * (rows + width), bytes_accessed=18 << 20, transcendentals=rows * width
        ),
        name="middle",
    )(acc, dense, outer, inner, pre_self, cotangent, w_neigh)


def per_device(
    features,
    w_self,
    w_neigh,
    local_tiles,
    local_rows,
    local_cols,
    halo_tiles,
    halo_rows,
    halo_cols,
    cut_rows,
    cut_counts,
    cotangent,
):
    row_count, width = features.shape
    tile_size = local_tiles.shape[1]
    n = lax.axis_size("rep")
    dom = lax.axis_size("dom")
    me = lax.axis_index("rep")
    blocks = row_count // tile_size
    assert n == 4
    first_out = [(0, 1), (3, 2), (1, 3), (2, 0)]
    second_out = [(0, 2), (3, 1), (1, 0), (2, 3)]
    first_in = [(b, a) for a, b in first_out]
    second_in = [(b, a) for a, b in second_out]
    swap_inner = [(1, 2), (2, 1)]
    outward, inward = [(1, 0), (2, 3)], [(0, 1), (3, 2)]

    def move(value, pairs):
        return lax.ppermute(value, "rep", pairs)

    half = row_count // 2
    low, high = features[:half], features[half:]
    second = move(features, second_in)
    first_a = move(low, first_in)
    first_b = move(high, first_in)
    inner_a, inner_b = move(low, swap_inner), move(high, swap_inner)

    slot = jnp.bitwise_xor(local_cols // blocks, me)
    crossed = ((me == 1) | (me == 2)) & ((slot == 1) | (slot == 2))
    slot = jnp.where(crossed, 3 - slot, slot)
    slot_cols = slot * blocks + local_cols % blocks
    cut_list = cut_rows[0, 0]
    halo_size = cut_list.shape[0] * cut_list.shape[1]
    parts, hdense = densify(
        local_tiles,
        local_rows,
        slot_cols,
        halo_tiles,
        halo_rows,
        halo_cols,
        row_count,
        n,
        halo_size,
    )

    def part(slot_id):
        return parts[slot_id]

    slot_index = jnp.arange(cut_list.shape[1], dtype=jnp.int32)
    live = slot_index[None, :] < cut_counts[0, 0][:, None]
    node_ids = jnp.arange(row_count, dtype=jnp.int32)
    selector = (
        (cut_list.reshape(-1)[:, None] == node_ids[None, :]) & live.reshape(-1)[:, None]
    ).astype(jnp.bfloat16)
    chosen = dot(selector, features).astype(jnp.bfloat16)
    incoming = lax.all_to_all(
        chosen.reshape(dom, -1, width), "dom", split_axis=0, concat_axis=0, tiled=True
    ).reshape(halo_size, width)

    pre_self = dot(features, w_self)
    summed = dot(part(0), features) + dot(hdense, incoming)
    third_a = move(first_a, outward)
    third_b = move(first_b, outward)
    summed = summed + dot(part(2), second)
    summed = summed + dot(part(1)[:, :half], first_a) + dot(part(1)[:, half:], first_b)
    summed = lax.optimization_barrier(summed)
    summed = summed + dot(part(3)[:, :half], third_a + inner_a)
    out, neighbour, grad_pre, grad_agg, term_a = middle(
        summed, part(3), third_b, inner_b, pre_self, cotangent, w_neigh
    )

    few = row_count // 2
    passed_a = move(term_a, inward)
    near_a = move(term_a, swap_inner)
    term_b = dot_t(part(3)[:, few:], grad_agg).astype(jnp.bfloat16)
    passed_b = move(term_b, inward)
    near_b = move(term_b, swap_inner)

    grad_scale = float(row_count * n * dom) ** (-0.5)
    share = width // (n * dom)
    d_self = (dot_t(features, grad_pre) * grad_scale).astype(jnp.bfloat16)
    d_neigh = (dot_t(neighbour, grad_pre) * grad_scale).astype(jnp.bfloat16)
    halo_back = dot_t(hdense, grad_agg).astype(jnp.bfloat16)
    both = jnp.stack([d_self, d_neigh]).reshape(2, n, dom, share, width)
    both = jnp.transpose(both, (2, 1, 0, 3, 4)).reshape(dom, 2 * n * share, width)
    both = jnp.concatenate([halo_back.reshape(dom, -1, width), both], axis=1)
    both = lax.all_to_all(both, "dom", split_axis=0, concat_axis=0, tiled=True)
    slots = cut_list.shape[1]
    returned = both[:, :slots].reshape(halo_size, width)
    both = jnp.sum(both[:, slots:].astype(jnp.float32), axis=0).reshape(n, 2, share, width)
    both = both.astype(jnp.bfloat16)
    both = lax.all_to_all(both, "rep", split_axis=0, concat_axis=0, tiled=True)
    both = jnp.sum(both.astype(jnp.float32), axis=0)
    both = jnp.broadcast_to(both[None], (dom, 2, share, width))
    both = lax.all_to_all(
        both,
        "dom",
        split_axis=0,
        concat_axis=0,
        tiled=True,
    )
    d_w_self = both[:, 0].reshape(width // n, width)
    d_w_neigh = both[:, 1].reshape(width // n, width)

    second_term = dot_t(part(2), grad_agg).astype(jnp.bfloat16)
    second_back = move(second_term, second_out)
    first_term = lax.optimization_barrier(dot_t(part(1), grad_agg))
    first_term = first_term + jnp.concatenate([passed_a, passed_b]).astype(jnp.float32)
    most = row_count - row_count // 4
    last_a = move(first_term[:most].astype(jnp.bfloat16), first_out)
    last_b = move(first_term[most:].astype(jnp.bfloat16), first_out)

    d_x = dot(grad_pre, w_self.T) + dot_t(part(0), grad_agg)
    d_x = d_x + jnp.concatenate([near_a, near_b]).astype(jnp.float32)
    d_x = d_x + dot_t(selector, returned)
    d_x = d_x + second_back.astype(jnp.float32)
    d_x = lax.optimization_barrier(d_x)
    base = jnp.concatenate([last_a.astype(jnp.float32), jnp.zeros((row_count - most, width))])
    base = lax.optimization_barrier((d_x + base).astype(jnp.bfloat16))
    last = (d_x[most:] + last_b.astype(jnp.float32)).astype(jnp.bfloat16)
    d_x = lax.dynamic_update_slice_in_dim(base, last, most, 0)
    return (out, d_x, d_w_self, d_w_neigh)


def solution(mesh):
    lead = ("dom", "rep")
    in_specs = (
        P(lead, None),
        P(),
        P(),
        P(lead, None, None),
        P(lead),
        P(lead),
        P(lead, None, None),
        P(lead),
        P(lead),
        P("dom", "rep", None, None),
        P("dom", "rep", None),
        P(lead, None),
    )
    out_specs = (P(lead, None), P(lead, None), P("rep", None), P("rep", None))

    return jax.shard_map(per_device, mesh=mesh, in_specs=in_specs, out_specs=out_specs, check_vma=False)
```
